512 devices in a mesh: band: 32 (over x, y_lo, core), grid: 16 (over z, y_hi).
Axes of the slice: x: 4, y: 8 (y_hi: 2, y_lo: 4; y = y_hi * 4 + y_lo), z: 8, core: 2. Of those that a mesh axis runs over, the one named last changes fastest.
Arguments:
- orbitals: bfloat16 [64, 160, 25600], P('band', 'grid'), may hold values from -6 to 6
- source_index: int32 [2], replicated, may hold values from 0 to 63
Outputs:
- fock_exchange: bfloat16 [64, 160, 25600], P('band', 'grid')
The draws below stay inside these ranges and needn't reach their ends.
All inputs are finite; a program needn't handle non-finite values.
Results may differ from the reference program's by a relative error of at most 0.012.
The reference program's roundings to bfloat16 on the way count: a program that leaves them out, or rounds other values in their place, can miss the bound.
Values may be sent and summed in bfloat16 or wider, within the bound.
A program may use at most 64 MiB of HBM per device.

```python
import math
import jax
import jax.numpy as jnp
from jax import lax

GRID = 160
NSRC = 2
ORBITALS = 64


def draw_orbitals(key, part):
    first_key = jax.random.fold_in(key, 0)
    shape_all = (ORBITALS, GRID, GRID * GRID)
    normal_part = jax.random.normal(first_key, shape_all, jnp.float32)
    return jnp.clip(normal_part, -6.0, 6.0).astype(jnp.bfloat16)


def setup_inputs(seed: int = 0) -> dict:
    streams_of = jax.random.split(jax.random.key(seed), 3)
    orbitals = draw_orbitals(jax.random.fold_in(streams_of[2], 71), 0)
    source_index = jax.random.randint(streams_of[1], (NSRC,), 0, ORBITALS).astype(jnp.int32)
    return dict(orbitals=orbitals, source_index=source_index)


spacing = 0.3

def cas_table(extent):
    wavenum = jnp.arange(extent, dtype=jnp.int32)
    products_mod = wavenum[:, None] * wavenum[None, :] % extent
    radians = products_mod.astype(jnp.float32) * (2.0 * math.pi / extent)
    return ((jnp.cos(radians) + jnp.sin(radians)) / math.sqrt(extent)).astype(jnp.bfloat16)

def wave_square(indices, extent):
    folded = jnp.minimum(indices, extent - indices).astype(jnp.float32)
    return folded * folded

def coulomb_table(extent):
    square_x = wave_square(jnp.arange(extent, dtype=jnp.int32), extent)
    total_sq = square_x[:, None, None] + square_x[None, :, None] + square_x[None, None, :]
    strength = (extent * spacing) ** 2 / math.pi
    return jnp.where(total_sq > 0, strength / (total_sq + 1.0), 0.0).astype(jnp.float32)

def along(grid_data, cas_matrix, which_axis):
    turned = jnp.tensordot(grid_data.astype(jnp.float32), cas_matrix.astype(jnp.float32), axes=([which_axis], [1]))
    return jnp.moveaxis(turned, -1, which_axis)

def reference(orbitals, source_index):
    grids = orbitals.reshape(ORBITALS, GRID, GRID, GRID)
    cas_matrix = cas_table(GRID)
    kernel = coulomb_table(GRID)
    sources = grids[source_index]

    def exchange_for(target_orbital):
        summed = jnp.zeros(target_orbital.shape, jnp.float32)
        for number in range(NSRC):
            source = sources[number].astype(jnp.float32)
            density = (source * target_orbital.astype(jnp.float32)).astype(jnp.bfloat16)
            along_z = along(density, cas_matrix, 2).astype(jnp.bfloat16)
            along_y = along(along_z, cas_matrix, 1).astype(jnp.bfloat16)
            scaled = (kernel * along(along_y, cas_matrix, 0)).astype(jnp.bfloat16)
            back_x = along(scaled, cas_matrix, 0).astype(jnp.bfloat16)
            again_y = along(back_x, cas_matrix, 1).astype(jnp.bfloat16)
            summed = summed + source * along(again_y, cas_matrix, 2)
        return (-summed).astype(jnp.bfloat16)
    result = lax.map(exchange_for, grids)
    return result.reshape(ORBITALS, GRID, GRID * GRID)
```

```python
import functools
import math

import jax
import jax.numpy as jnp
import ml_dtypes
import numpy as np
from jax import lax
from jax.experimental import pallas as pl
from jax.experimental.pallas import tpu as pltpu
from jax.sharding import PartitionSpec as P

MESH = pl.DeviceIdType.MESH
F32 = jnp.float32
BF16 = jnp.bfloat16

SPACING = 0.3
N = 160
NX = 10
NSRC = 2
NORB = 2
NGRID = 16
LANES = 128
REST = N - LANES
HALF = N // 2
GROUPS = N // 16
PAIRROWS = NX * 16
GRANULES = NORB * GROUPS + GROUPS // 2
SLAB = NX * N * N // LANES
PADDED = 2048
PIECE = PADDED // 8
STEP = 9


def tables():
    k = np.arange(N)
    radians = ((k[:, None] * k[None, :]) % N).astype(np.float32) * np.float32(2.0 * math.pi / N)
    cas = ((np.cos(radians) + np.sin(radians)) / np.float32(math.sqrt(N))).astype(ml_dtypes.bfloat16)
    cas = cas.astype(np.float32)
    order = np.array([4 * (r % 40) + r // 40 for r in range(N)])
    y_in = cas[:, order]
    y_out = cas[order, :]
    z_in = np.zeros((NORB, 4, 2, LANES, 2 * LANES), np.float32)
    z_out = np.zeros((NORB, 4, 2 * LANES, 2 * LANES), np.float32)
    for l in range(NORB):
        place = np.zeros((N, 2 * LANES), np.float32)
        place[:, :LANES] = cas[:, :LANES]
        for q in range(2):
            at = LANES + 64 * l + 32 * q
            place[:, at : at + REST] = cas[:, LANES:]
        back = np.zeros((2 * LANES, N), np.float32)
        back[:LANES] = cas[:LANES]
        back[LANES + 64 * l : LANES + 64 * l + REST] = cas[LANES:]
        for i in range(4):
            for part in range(2):
                for lane in range(LANES):
                    z = lane + LANES * (i + part) - N * i
                    if 0 <= z < N:
                        z_in[l, i, part, lane] = place[z]
                        z_out[l, i, :, LANES * part + lane] = back[:, z]
    return [t.astype(ml_dtypes.bfloat16) for t in (cas, y_in, y_out, z_in, z_out)]


def dot(a, b):
    return jnp.dot(a, b, preferred_element_type=F32)


def squares(index):
    folded = jnp.minimum(index, N - index).astype(F32)
    return folded * folded


def body(
    orb, con, cas, y_in, y_out, z_in, z_out, out,
    buf1, buf2, src, srcf, dens, srcd, mid, send, recv, work, ready, back, table, outf,
    s1, s2, s3, sf, sb, r1, r2, r3, rf, rb,
):
    band = lax.axis_index("band")
    me = lax.axis_index("grid")
    x_at = band // 8
    y_at = lax.rem(band // 2, 4)
    core = lax.rem(band, 2)
    q_me = x_at * 2 + core

    def at_q(q):
        return ((q // 2) * 8 + y_at * 2 + lax.rem(q, 2), me)

    def at_y(y):
        return (x_at * 8 + y * 2 + core, me)

    def at_grid(t):
        return (band, t)

    barrier = pltpu.get_barrier_semaphore()

    def hello(device):
        pl.semaphore_signal(barrier, inc=1, device_id=device, device_id_type=MESH)

    for k in range(1, 8):
        hello(at_q(lax.rem(q_me + k, 8)))
    for k in range(1, 4):
        hello(at_y(lax.rem(y_at + k, 4)))
    for k in range(1, NGRID):
        hello(at_grid(lax.rem(me + k, NGRID)))
    pl.semaphore_wait(barrier, 7 + 3 + NGRID - 1)

    def rows(q):
        return pl.ds(pl.multiple_of(q * PIECE, PIECE), PIECE)

    def first(j, k):
        q = lax.rem(q_me + k, 8)
        return pltpu.make_async_remote_copy(
            con.at[j, rows(q)], buf1.at[j, q_me], s1.at[j, k], r1.at[j],
            device_id=at_q(q), device_id_type=MESH)

    def second(j, k):
        y = lax.rem(y_at + k, 4)
        return pltpu.make_async_remote_copy(
            buf2.at[j, y_at], buf2.at[j, y_at], s2.at[j, k], r2.at[j],
            device_id=at_y(y), device_id_type=MESH)

    def third(j, k):
        q = lax.rem(q_me + k, 8)
        return pltpu.make_async_remote_copy(
            src.at[j, rows(q_me)], src.at[j, rows(q_me)], s3.at[j, k], r3.at[j],
            device_id=at_q(q), device_id_type=MESH)

    for j in range(NSRC):
        for k in range(1, 8):
            first(j, k).start()
    for j in range(NSRC):
        buf1[j, q_me] = con[j, rows(q_me), :]

    def granule(j, slot):
        return lax.rem(me + (NGRID - STEP) * j, NGRID) + NGRID * slot

    lane = lax.broadcasted_iota(jnp.int32, (1, LANES), 1)
    kx = squares(lax.broadcasted_iota(jnp.int32, (N, LANES), 0))
    strength = (N * SPACING) ** 2 / math.pi
    for j in range(NSRC):
        for slot in range(2):
            g = granule(j, slot)

            def fill(r, _, g=g, at=2 * j + slot):
                plain = jnp.zeros((1, LANES), jnp.int32) + (16 * lax.rem(g, GROUPS) + r)
                folded = HALF * lax.rem(lane // 32, 2) + (16 * (g - NORB * GROUPS) + r)
                rest = g >= NORB * GROUPS
                ky = jnp.where(rest, folded, plain)
                kz = jnp.where(rest, LANES + lax.rem(lane, 32), lane)
                total = kx + (squares(ky) + squares(kz))
                table[at, r] = jnp.where(total > 0, strength / (total + 1.0), 0.0)
                return 0

            lax.fori_loop(0, 16, fill, 0)

    for j in range(NSRC):
        got = buf1.at[j, pl.ds(0, 7)]
        pltpu.make_async_copy(got, got, r1.at[j]).wait()
        buf2[j, y_at] = jnp.sum(buf1[j].astype(F32), axis=0).astype(BF16)
        for k in range(1, 4):
            second(j, k).start()
    for j in range(NSRC):
        got = buf2.at[j, pl.ds(0, 3)]
        pltpu.make_async_copy(got, got, r2.at[j]).wait()
        src[j, rows(q_me), :] = jnp.sum(buf2[j].astype(F32), axis=0).astype(BF16)
        for k in range(1, 8):
            third(j, k).start()

    zone = lax.rem(lane // 32, 2) == 0

    def order(j, k):
        g = lax.rem(7 * k + 3 * me + 12 * core, GRANULES)
        t = lax.rem(g + STEP * j, NGRID)
        return g, t

    def forward(j, k):
        g, t = order(j, k)
        return t, pltpu.make_async_remote_copy(
            send.at[j, g], recv.at[j, g // NGRID, me], sf.at[j, k], rf.at[j, g // NGRID],
            device_id=at_grid(t), device_id_type=MESH)

    def forward_own(j, k):
        g, t = order(j, k)
        return pltpu.make_async_copy(send.at[j, g], recv.at[j, g // NGRID, me], rf.at[j, g // NGRID])

    for j in range(NSRC):
        got = src.at[j, pl.ds(0, 7 * PIECE)]
        pltpu.make_async_copy(got, got, r3.at[j]).wait()
        srcf[...] = src[j].astype(F32)

        def spread(x, _, j=j):
            at = pl.ds(pl.multiple_of(x * 40, 8), 40)
            for m in range(5):
                s = srcf[pl.ds(x * 200 + m, 40, stride=5), :]
                srcd[j, m, at, :] = s
                for l in range(NORB):
                    dens[l, m, at, :] = s * orb[l, pl.ds(x * 200 + m, 40, stride=5), :]
            return 0

        lax.fori_loop(0, NX, spread, 0)
        for i in range(4):
            parts = []
            for l in range(NORB):
                t = dot(dens[l, i].astype(BF16), z_in[l, i, 0]) + dot(dens[l, i + 1].astype(BF16), z_in[l, i, 1])
                mid[l, i] = t[:, :LANES]
                parts.append(t[:, LANES:])
            mid[NORB, i] = parts[0] + parts[1]

        def along_y(x, _, j=j):
            at = pl.ds(pl.multiple_of(x * 40, 8), 40)
            to = pl.ds(pl.multiple_of(x * 16, 16), 16)
            cols = [
                jnp.concatenate([mid[l, i, at, :] for i in range(4)], axis=0).astype(BF16)
                for l in range(NORB + 1)
            ]
            o = dot(y_in[...], jnp.concatenate(cols, axis=1))
            for l in range(NORB):
                for g in range(GROUPS):
                    send[j, l * GROUPS + g, to, :] = o[16 * g : 16 * g + 16, LANES * l : LANES * (l + 1)].astype(BF16)
            last = o[:, NORB * LANES :]
            both = jnp.where(zone, last[:HALF], last[HALF:])
            for g in range(GROUPS // 2):
                send[j, NORB * GROUPS + g, to, :] = both[16 * g : 16 * g + 16].astype(BF16)
            return 0

        lax.fori_loop(0, NX, along_y, 0)

        def post(k, _, j=j):
            t, copy = forward(j, k)

            @pl.when(t == me)
            def _():
                forward_own(j, k).start()

            @pl.when(t != me)
            def _():
                copy.start()

            return 0

        lax.fori_loop(0, GRANULES, post, 0)

    def reply(j, slot, k):
        t = lax.rem(me + k, NGRID)
        return pltpu.make_async_remote_copy(
            ready.at[j, slot, t], back.at[j, granule(j, slot)], sb.at[j, slot, k], rb.at[j],
            device_id=at_grid(t), device_id_type=MESH)

    def reply_own(j, slot):
        return pltpu.make_async_copy(ready.at[j, slot, me], back.at[j, granule(j, slot)], rb.at[j])

    def along_x(j, slot):
        got = recv.at[j, slot]
        pltpu.make_async_copy(got, got, rf.at[j, slot]).wait()
        work[...] = recv[j, slot].reshape(NGRID * PAIRROWS, LANES).astype(F32)

        def two(h, _):
            one = pl.ds(2 * h, N, stride=16)
            other = pl.ds(2 * h + 1, N, stride=16)
            f = jnp.concatenate([work[one, :].astype(BF16), work[other, :].astype(BF16)], axis=1)
            u = dot(cas[...], f)
            scale = jnp.concatenate([table[2 * j + slot, 2 * h], table[2 * j + slot, 2 * h + 1]], axis=1)
            v = dot(cas[...], (scale * u).astype(BF16))
            work[one, :] = v[:, :LANES]
            work[other, :] = v[:, LANES:]
            return 0

        lax.fori_loop(0, 8, two, 0)
        ready[j, slot] = work[...].astype(BF16).reshape(NGRID, PAIRROWS, LANES)
        reply_own(j, slot).start()
        for k in range(1, NGRID):
            reply(j, slot, k).start()

    for j in range(NSRC):
        along_x(j, 0)

        @pl.when(granule(j, 1) < GRANULES)
        def _(j=j):
            along_x(j, 1)

    for j in range(NSRC):
        got = back.at[j]
        pltpu.make_async_copy(got, got, rb.at[j]).wait()

        def again_y(x, _, j=j):
            at = pl.ds(pl.multiple_of(x * 40, 8), 40)
            to = pl.ds(pl.multiple_of(x * 16, 16), 16)
            cols = [back[j, pl.ds(l * GROUPS, GROUPS), to, :].reshape(N, LANES) for l in range(NORB)]
            b = back[j, pl.ds(NORB * GROUPS, GROUPS // 2), to, :].reshape(HALF, LANES)
            turned = pltpu.roll(b.astype(F32), LANES - 32, 1).astype(BF16)
            cols.append(jnp.concatenate([b, turned], axis=0))
            o = dot(y_out[...], jnp.concatenate(cols, axis=1))
            for l in range(NORB + 1):
                for i in range(4):
                    mid[l, i, at, :] = o[40 * i : 40 * i + 40, LANES * l : LANES * (l + 1)]
            return 0

        lax.fori_loop(0, NX, again_y, 0)
        for l in range(NORB):
            left = None
            for i in range(4):
                f = jnp.concatenate([mid[l, i].astype(BF16), mid[NORB, i].astype(BF16)], axis=1)
                t = dot(f, z_out[l, i])
                here = t[:, :LANES] if left is None else left + t[:, :LANES]
                left = t[:, LANES:]
                dens[l, i] = srcd[j, i] * here if j == 0 else dens[l, i] + srcd[j, i] * here
            dens[l, 4] = srcd[j, 4] * left if j == 0 else dens[l, 4] + srcd[j, 4] * left

    def gather(x, _):
        at = pl.ds(pl.multiple_of(x * 40, 8), 40)
        for l in range(NORB):
            for m in range(5):
                outf[l, pl.ds(x * 200 + m, 40, stride=5), :] = -dens[l, m, at, :]
        return 0

    lax.fori_loop(0, NX, gather, 0)
    out[...] = outf[...].astype(BF16)

    for j in range(NSRC):
        for k in range(1, 8):
            first(j, k).wait_send()
            third(j, k).wait_send()
        for k in range(1, 4):
            second(j, k).wait_send()

        def posted(k, _, j=j):
            t, copy = forward(j, k)

            @pl.when(t != me)
            def _():
                copy.wait_send()

            return 0

        lax.fori_loop(0, GRANULES, posted, 0)
        for slot in range(2):

            @pl.when(granule(j, slot) < GRANULES)
            def _(j=j, slot=slot):
                for k in range(1, NGRID):
                    reply(j, slot, k).wait_send()


def exchange(orb, con):
    consts = [jnp.asarray(t) for t in tables()]
    vmem = pl.BlockSpec(memory_space=pltpu.VMEM)
    dma = pltpu.SemaphoreType.DMA
    return pl.pallas_call(
        body,
        out_shape=jax.ShapeDtypeStruct((NORB, SLAB, LANES), BF16),
        in_specs=[vmem] * (2 + len(consts)),
        out_specs=vmem,
        scratch_shapes=[
            pltpu.VMEM((NSRC, 8, PIECE, LANES), BF16),
            pltpu.VMEM((NSRC, 4, PIECE, LANES), BF16),
            pltpu.VMEM((NSRC, PADDED, LANES), BF16),
            pltpu.VMEM((PADDED, LANES), F32),
            pltpu.VMEM((NORB, 5, 40 * NX, LANES), F32),
            pltpu.VMEM((NSRC, 5, 40 * NX, LANES), F32),
            pltpu.VMEM((NORB + 1, 4, 40 * NX, LANES), F32),
            pltpu.VMEM((NSRC, GRANULES, PAIRROWS, LANES), BF16),
            pltpu.VMEM((NSRC, 2, NGRID, PAIRROWS, LANES), BF16),
            pltpu.VMEM((NGRID * PAIRROWS, LANES), F32),
            pltpu.VMEM((NSRC, 2, NGRID, PAIRROWS, LANES), BF16),
            pltpu.VMEM((NSRC, GRANULES, PAIRROWS, LANES), BF16),
            pltpu.VMEM((2 * NSRC, 16, N, LANES), F32),
            pltpu.VMEM((NORB, SLAB, LANES), F32),
            dma((NSRC, 8)),
            dma((NSRC, 4)),
            dma((NSRC, 8)),
            dma((NSRC, GRANULES)),
            dma((NSRC, 2, NGRID)),
            dma((NSRC,)),
            dma((NSRC,)),
            dma((NSRC,)),
            dma((NSRC, 2)),
            dma((NSRC,)),
        ],
        compiler_params=pltpu.CompilerParams(
            collective_id=0, has_side_effects=True, vmem_limit_bytes=56 << 20
        ),
        name="exchange",
    )(orb, con, *consts)


def shards(orbitals, source_index):
    local = orbitals.shape[0]
    flat = orbitals.reshape(local, SLAB, LANES)
    band = lax.axis_index("band")
    parts = []
    for j in range(NSRC):
        slab = lax.dynamic_index_in_dim(flat, source_index[j] % local, 0, keepdims=False)
        parts.append(jnp.where(band == source_index[j] // local, slab, jnp.zeros_like(slab)))
    con = jnp.pad(jnp.stack(parts), ((0, 0), (0, PADDED - SLAB), (0, 0)))
    result = exchange(flat.astype(F32), con)
    return result.reshape(orbitals.shape)


def solution(mesh):
    return jax.shard_map(
        shards,
        mesh=mesh,
        in_specs=(P("band", "grid", None), P()),
        out_specs=P("band", "grid", None),
        check_vma=False,
    )
```

```python
import math

import jax
import jax.numpy as jnp
import ml_dtypes
import numpy as np
from jax import lax
from jax.experimental import pallas as pl
from jax.experimental.pallas import tpu as pltpu
from jax.sharding import PartitionSpec as P

MESH = pl.DeviceIdType.MESH
F32 = jnp.float32
BF16 = jnp.bfloat16

SPACING = 0.3
N = 160
NX = 10
NSRC = 2
NORB = 2
NGRID = 16
LANES = 128
REST = N - LANES
HALF = N // 2
GROUPS = N // 16
PAIRROWS = NX * 16
GRANULES = NORB * GROUPS + GROUPS // 2
SLAB = NX * N * N // LANES
PADDED = 2048
PIECE = PADDED // 8
STEP = 9


def tables():
    k = np.arange(N)
    radians = ((k[:, None] * k[None, :]) % N).astype(np.float32) * np.float32(2.0 * math.pi / N)
    cas = ((np.cos(radians) + np.sin(radians)) / np.float32(math.sqrt(N))).astype(ml_dtypes.bfloat16)
    cas = cas.astype(np.float32)
    order = np.array([4 * (r % 40) + r // 40 for r in range(N)])
    y_in = cas[:, order]
    y_out = cas[order, :]
    z_in = np.zeros((NORB, 4, 2, LANES, 2 * LANES), np.float32)
    z_out = np.zeros((NORB, 4, 2 * LANES, 2 * LANES), np.float32)
    for l in range(NORB):
        place = np.zeros((N, 2 * LANES), np.float32)
        place[:, :LANES] = cas[:, :LANES]
        for q in range(2):
            at = LANES + 64 * l + 32 * q
            place[:, at : at + REST] = cas[:, LANES:]
        back = np.zeros((2 * LANES, N), np.float32)
        back[:LANES] = cas[:LANES]
        back[LANES + 64 * l : LANES + 64 * l + REST] = cas[LANES:]
        for i in range(4):
            for part in range(2):
                for lane in range(LANES):
                    z = lane + LANES * (i + part) - N * i
                    if 0 <= z < N:
                        z_in[l, i, part, lane] = place[z]
                        z_out[l, i, :, LANES * part + lane] = back[:, z]
    return [t.astype(ml_dtypes.bfloat16) for t in (cas, y_in, y_out, z_in, z_out)]


def dot(a, b):
    return jnp.dot(a, b, preferred_element_type=F32)


def squares(index):
    folded = jnp.minimum(index, N - index).astype(F32)
    return folded * folded


def body(
    index, orb, cas, y_in, y_out, z_in, z_out, out,
    flat, con, buf1, buf2, src, srcf, dens, srcd, mid, send, recv, work, ready, back, table,
    s1, s2, s3, sf, sb, r1, r2, r3, rf, rb,
):
    band = lax.axis_index("band")
    me = lax.axis_index("grid")
    x_at = band // 8
    y_at = lax.rem(band // 2, 4)
    core = lax.rem(band, 2)
    q_me = x_at * 2 + core

    def at_q(q):
        return ((q // 2) * 8 + y_at * 2 + lax.rem(q, 2), me)

    def at_y(y):
        return (x_at * 8 + y * 2 + core, me)

    def at_grid(t):
        return (band, t)

    barrier = pltpu.get_barrier_semaphore()

    def hello(device):
        pl.semaphore_signal(barrier, inc=1, device_id=device, device_id_type=MESH)

    for k in range(1, 8):
        hello(at_q(lax.rem(q_me + k, 8)))
    for k in range(1, 4):
        hello(at_y(lax.rem(y_at + k, 4)))
    for k in range(1, NGRID):
        hello(at_grid(lax.rem(me + k, NGRID)))

    flat[...] = orb[...].astype(F32).reshape(NORB * SLAB, LANES)
    for j in range(NSRC):
        mine = [jnp.where(index[j] == NORB * band + l, 1.0, 0.0) for l in range(NORB)]

        def share(h, _, j=j, mine=mine):
            part = sum(
                mine[l] * flat[pl.ds(h * NORB * 400 + l, 400, stride=NORB), :] for l in range(NORB)
            )
            con[j, pl.ds(pl.multiple_of(h * 400, 16), 400), :] = part.astype(BF16)
            return 0

        lax.fori_loop(0, SLAB // 400, share, 0)
        con[j, SLAB:, :] = jnp.zeros((PADDED - SLAB, LANES), BF16)

    def granule(j, slot):
        return lax.rem(me + (NGRID - STEP) * j, NGRID) + NGRID * slot

    lane = lax.broadcasted_iota(jnp.int32, (1, LANES), 1)
    kx = squares(lax.broadcasted_iota(jnp.int32, (N, LANES), 0))
    strength = (N * SPACING) ** 2 / math.pi
    for j in range(NSRC):
        for slot in range(2):
            g = granule(j, slot)

            def fill(r, _, g=g, at=2 * j + slot):
                plain = jnp.zeros((1, LANES), jnp.int32) + (16 * lax.rem(g, GROUPS) + r)
                folded = HALF * lax.rem(lane // 32, 2) + (16 * (g - NORB * GROUPS) + r)
                rest = g >= NORB * GROUPS
                ky = jnp.where(rest, folded, plain)
                kz = jnp.where(rest, LANES + lax.rem(lane, 32), lane)
                total = kx + (squares(ky) + squares(kz))
                table[at, r] = jnp.where(total > 0, strength / (total + 1.0), 0.0)
                return 0

            lax.fori_loop(0, 16, fill, 0)

    pl.semaphore_wait(barrier, 7 + 3 + NGRID - 1)

    def rows(q):
        return pl.ds(pl.multiple_of(q * PIECE, PIECE), PIECE)

    def first(j, k):
        q = lax.rem(q_me + k, 8)
        return pltpu.make_async_remote_copy(
            con.at[j, rows(q)], buf1.at[j, q_me], s1.at[j, k], r1.at[j],
            device_id=at_q(q), device_id_type=MESH)

    def second(j, k):
        y = lax.rem(y_at + k, 4)
        return pltpu.make_async_remote_copy(
            buf2.at[j, y_at], buf2.at[j, y_at], s2.at[j, k], r2.at[j],
            device_id=at_y(y), device_id_type=MESH)

    def third(j, k):
        q = lax.rem(q_me + k, 8)
        return pltpu.make_async_remote_copy(
            src.at[j, rows(q_me)], src.at[j, rows(q_me)], s3.at[j, k], r3.at[j],
            device_id=at_q(q), device_id_type=MESH)

    def begin(j):
        for k in range(1, 8):
            first(j, k).start()
        buf1[j, q_me] = con[j, rows(q_me), :]

    def middle(j):
        got = buf1.at[j, pl.ds(0, 7)]
        pltpu.make_async_copy(got, got, r1.at[j]).wait()
        buf2[j, y_at] = jnp.sum(buf1[j].astype(F32), axis=0).astype(BF16)
        for k in range(1, 4):
            second(j, k).start()

    def end(j):
        got = buf2.at[j, pl.ds(0, 3)]
        pltpu.make_async_copy(got, got, r2.at[j]).wait()
        src[j, rows(q_me), :] = jnp.sum(buf2[j].astype(F32), axis=0).astype(BF16)
        for k in range(1, 8):
            third(j, k).start()

    begin(0)
    middle(0)
    begin(1)
    end(0)
    middle(1)
    end(1)

    zone = lax.rem(lane // 32, 2) == 0

    def order(j, k):
        turn = 2 * me + 5 * core + 3 * y_at
        low = lax.rem(7 * k + turn, NGRID)
        high = NGRID + lax.rem(2 * k + turn, GRANULES - NGRID)
        g = jnp.where(k < NGRID, low, high)
        t = lax.rem(g + STEP * j, NGRID)
        return g, t

    def forward(j, k):
        g, t = order(j, k)
        return t, pltpu.make_async_remote_copy(
            send.at[j, g], recv.at[j, g // NGRID, me], sf.at[j, k], rf.at[j, g // NGRID],
            device_id=at_grid(t), device_id_type=MESH)

    def forward_own(j, k):
        g, t = order(j, k)
        return pltpu.make_async_copy(send.at[j, g], recv.at[j, g // NGRID, me], rf.at[j, g // NGRID])

    for j in range(NSRC):
        got = src.at[j, pl.ds(0, 7 * PIECE)]
        pltpu.make_async_copy(got, got, r3.at[j]).wait()
        srcf[...] = src[j].astype(F32)

        def spread(x, _, j=j):
            at = pl.ds(pl.multiple_of(x * 40, 8), 40)
            for m in range(5):
                s = srcf[pl.ds(x * 200 + m, 40, stride=5), :]
                srcd[j, m, at, :] = s
                for l in range(NORB):
                    dens[l, m, at, :] = s * flat[pl.ds(NORB * (x * 200 + m) + l, 40, stride=5 * NORB), :]
            return 0

        lax.fori_loop(0, NX, spread, 0)
        for i in range(4):
            parts = []
            for l in range(NORB):
                t = dot(dens[l, i].astype(BF16), z_in[l, i, 0]) + dot(dens[l, i + 1].astype(BF16), z_in[l, i, 1])
                mid[l, i] = t[:, :LANES]
                parts.append(t[:, LANES:])
            mid[NORB, i] = parts[0] + parts[1]

        def along_y(x, _, j=j):
            at = pl.ds(pl.multiple_of(x * 40, 8), 40)
            to = pl.ds(pl.multiple_of(x * 16, 16), 16)
            cols = [
                jnp.concatenate([mid[l, i, at, :] for i in range(4)], axis=0).astype(BF16)
                for l in range(NORB + 1)
            ]
            o = dot(y_in[...], jnp.concatenate(cols, axis=1))
            for l in range(NORB):
                for g in range(GROUPS):
                    send[j, l * GROUPS + g, to, :] = o[16 * g : 16 * g + 16, LANES * l : LANES * (l + 1)].astype(BF16)
            last = o[:, NORB * LANES :]
            both = jnp.where(zone, last[:HALF], last[HALF:])
            for g in range(GROUPS // 2):
                send[j, NORB * GROUPS + g, to, :] = both[16 * g : 16 * g + 16].astype(BF16)
            return 0

        lax.fori_loop(0, NX, along_y, 0)

        def post(k, _, j=j):
            t, copy = forward(j, k)

            @pl.when(t == me)
            def _():
                forward_own(j, k).start()

            @pl.when(t != me)
            def _():
                copy.start()

            return 0

        lax.fori_loop(0, GRANULES, post, 0)

    def reply(j, slot, k):
        t = lax.rem(7 * k + 2 * me + 5 * core + 3 * y_at, NGRID)
        return t, pltpu.make_async_remote_copy(
            ready.at[j, slot, t], back.at[j, granule(j, slot)], sb.at[j, slot, k], rb.at[j],
            device_id=at_grid(t), device_id_type=MESH)

    def reply_own(j, slot):
        return pltpu.make_async_copy(ready.at[j, slot, me], back.at[j, granule(j, slot)], rb.at[j])

    def along_x(j, slot):
        got = recv.at[j, slot]
        pltpu.make_async_copy(got, got, rf.at[j, slot]).wait()
        work[...] = recv[j, slot].reshape(NGRID * PAIRROWS, LANES).astype(F32)

        def two(h, _):
            one = pl.ds(2 * h, N, stride=16)
            other = pl.ds(2 * h + 1, N, stride=16)
            f = jnp.concatenate([work[one, :].astype(BF16), work[other, :].astype(BF16)], axis=1)
            u = dot(cas[...], f)
            scale = jnp.concatenate([table[2 * j + slot, 2 * h], table[2 * j + slot, 2 * h + 1]], axis=1)
            v = dot(cas[...], (scale * u).astype(BF16))
            work[one, :] = v[:, :LANES]
            work[other, :] = v[:, LANES:]
            return 0

        lax.fori_loop(0, 8, two, 0)
        ready[j, slot] = work[...].astype(BF16).reshape(NGRID, PAIRROWS, LANES)

        def answer(k, _):
            t, copy = reply(j, slot, k)

            @pl.when(t == me)
            def _():
                reply_own(j, slot).start()

            @pl.when(t != me)
            def _():
                copy.start()

            return 0

        lax.fori_loop(0, NGRID, answer, 0)

    for j in range(NSRC):
        along_x(j, 0)

        @pl.when(granule(j, 1) < GRANULES)
        def _(j=j):
            along_x(j, 1)

    for j in range(NSRC):
        got = back.at[j]
        pltpu.make_async_copy(got, got, rb.at[j]).wait()

        def again_y(x, _, j=j):
            at = pl.ds(pl.multiple_of(x * 40, 8), 40)
            to = pl.ds(pl.multiple_of(x * 16, 16), 16)
            cols = [back[j, pl.ds(l * GROUPS, GROUPS), to, :].reshape(N, LANES) for l in range(NORB)]
            b = back[j, pl.ds(NORB * GROUPS, GROUPS // 2), to, :].reshape(HALF, LANES)
            turned = pltpu.roll(b.astype(F32), LANES - 32, 1).astype(BF16)
            cols.append(jnp.concatenate([b, turned], axis=0))
            o = dot(y_out[...], jnp.concatenate(cols, axis=1))
            for l in range(NORB + 1):
                for i in range(4):
                    mid[l, i, at, :] = o[40 * i : 40 * i + 40, LANES * l : LANES * (l + 1)]
            return 0

        lax.fori_loop(0, NX, again_y, 0)
        for l in range(NORB):
            left = None
            for i in range(4):
                f = jnp.concatenate([mid[l, i].astype(BF16), mid[NORB, i].astype(BF16)], axis=1)
                t = dot(f, z_out[l, i])
                here = t[:, :LANES] if left is None else left + t[:, :LANES]
                left = t[:, LANES:]
                dens[l, i] = srcd[j, i] * here if j == 0 else dens[l, i] + srcd[j, i] * here
            dens[l, 4] = srcd[j, 4] * left if j == 0 else dens[l, 4] + srcd[j, 4] * left

    def gather(x, _):
        at = pl.ds(pl.multiple_of(x * 40, 8), 40)
        for l in range(NORB):
            for m in range(5):
                flat[pl.ds(NORB * (x * 200 + m) + l, 40, stride=5 * NORB), :] = -dens[l, m, at, :]
        return 0

    lax.fori_loop(0, NX, gather, 0)
    out[...] = flat[...].reshape(SLAB, NORB, LANES).astype(BF16)

    for j in range(NSRC):
        for k in range(1, 8):
            first(j, k).wait_send()
            third(j, k).wait_send()
        for k in range(1, 4):
            second(j, k).wait_send()

        def posted(k, _, j=j):
            t, copy = forward(j, k)

            @pl.when(t != me)
            def _():
                copy.wait_send()

            return 0

        lax.fori_loop(0, GRANULES, posted, 0)
        for slot in range(2):

            @pl.when(granule(j, slot) < GRANULES)
            def _(j=j, slot=slot):
                def answered(k, _):
                    t, copy = reply(j, slot, k)

                    @pl.when(t != me)
                    def _():
                        copy.wait_send()

                    return 0

                lax.fori_loop(0, NGRID, answered, 0)


def exchange(index, orb):
    consts = [jnp.asarray(t) for t in tables()]
    vmem = pl.BlockSpec(memory_space=pltpu.VMEM)
    dma = pltpu.SemaphoreType.DMA
    return pl.pallas_call(
        body,
        out_shape=jax.ShapeDtypeStruct((SLAB, NORB, LANES), BF16),
        in_specs=[pl.BlockSpec(memory_space=pltpu.SMEM)] + [vmem] * (1 + len(consts)),
        out_specs=vmem,
        scratch_shapes=[
            pltpu.VMEM((NORB * SLAB, LANES), F32),
            pltpu.VMEM((NSRC, PADDED, LANES), BF16),
            pltpu.VMEM((NSRC, 8, PIECE, LANES), BF16),
            pltpu.VMEM((NSRC, 4, PIECE, LANES), BF16),
            pltpu.VMEM((NSRC, PADDED, LANES), BF16),
            pltpu.VMEM((PADDED, LANES), F32),
            pltpu.VMEM((NORB, 5, 40 * NX, LANES), F32),
            pltpu.VMEM((NSRC, 5, 40 * NX, LANES), F32),
            pltpu.VMEM((NORB + 1, 4, 40 * NX, LANES), F32),
            pltpu.VMEM((NSRC, GRANULES, PAIRROWS, LANES), BF16),
            pltpu.VMEM((NSRC, 2, NGRID, PAIRROWS, LANES), BF16),
            pltpu.VMEM((NGRID * PAIRROWS, LANES), F32),
            pltpu.VMEM((NSRC, 2, NGRID, PAIRROWS, LANES), BF16),
            pltpu.VMEM((NSRC, GRANULES, PAIRROWS, LANES), BF16),
            pltpu.VMEM((2 * NSRC, 16, N, LANES), F32),
            dma((NSRC, 8)),
            dma((NSRC, 4)),
            dma((NSRC, 8)),
            dma((NSRC, GRANULES)),
            dma((NSRC, 2, NGRID)),
            dma((NSRC,)),
            dma((NSRC,)),
            dma((NSRC,)),
            dma((NSRC, 2)),
            dma((NSRC,)),
        ],
        compiler_params=pltpu.CompilerParams(
            collective_id=0, has_side_effects=True, vmem_limit_bytes=56 << 20
        ),
        name="exchange",
    )(index, orb, *consts)


def shards(orbitals, source_index):
    rows = orbitals.reshape(NORB, SLAB, LANES).transpose(1, 0, 2)
    result = exchange(source_index, rows)
    return result.transpose(1, 0, 2).reshape(orbitals.shape)


def solution(mesh):
    return jax.shard_map(
        shards,
        mesh=mesh,
        in_specs=(P("band", "grid", None), P()),
        out_specs=P("band", "grid", None),
        check_vma=False,
    )
```

```python
import math

import jax
import jax.numpy as jnp
import ml_dtypes
import numpy as np
from jax import lax
from jax.experimental import pallas as pl
from jax.experimental.pallas import tpu as pltpu
from jax.sharding import PartitionSpec as P

MESH = pl.DeviceIdType.MESH
F32 = jnp.float32
BF16 = jnp.bfloat16

SPACING = 0.3
N = 160
NX = 10
NSRC = 2
NORB = 2
NGRID = 16
LANES = 128
REST = N - LANES
HALF = N // 2
GROUPS = N // 16
PAIRROWS = NX * 16
GRANULES = NORB * GROUPS + GROUPS // 2
SLAB = NX * N * N // LANES
PADDED = 2048
PIECE = PADDED // 8
STEP = 9


def tables():
    k = np.arange(N)
    radians = ((k[:, None] * k[None, :]) % N).astype(np.float32) * np.float32(2.0 * math.pi / N)
    cas = ((np.cos(radians) + np.sin(radians)) / np.float32(math.sqrt(N))).astype(ml_dtypes.bfloat16)
    cas = cas.astype(np.float32)
    order = np.array([4 * (r % 40) + r // 40 for r in range(N)])
    y_in = cas[:, order]
    y_out = cas[order, :]
    z_in = np.zeros((NORB, 4, 2, LANES, 2 * LANES), np.float32)
    z_out = np.zeros((NORB, 4, 2 * LANES, 2 * LANES), np.float32)
    for l in range(NORB):
        place = np.zeros((N, 2 * LANES), np.float32)
        place[:, :LANES] = cas[:, :LANES]
        for q in range(2):
            at = LANES + 64 * l + 32 * q
            place[:, at : at + REST] = cas[:, LANES:]
        back = np.zeros((2 * LANES, N), np.float32)
        back[:LANES] = cas[:LANES]
        back[LANES + 64 * l : LANES + 64 * l + REST] = cas[LANES:]
        for i in range(4):
            for part in range(2):
                for lane in range(LANES):
                    z = lane + LANES * (i + part) - N * i
                    if 0 <= z < N:
                        z_in[l, i, part, lane] = place[z]
                        z_out[l, i, :, LANES * part + lane] = back[:, z]
    return [t.astype(ml_dtypes.bfloat16) for t in (cas, y_in, y_out, z_in, z_out)]


def dot(a, b):
    return jnp.dot(a, b, preferred_element_type=F32)


def squares(index):
    folded = jnp.minimum(index, N - index).astype(F32)
    return folded * folded


def body(
    index, orb, cas, y_in, y_out, z_in, z_out, out,
    flat, orbd, con, bufd, pair, buf1, buf2, src, dens, total, mid, send, recv, work, ready, back, table,
    sd, s1, s2, s3, se, sf, sb, rd, r1, r2, r3, re, rf, rb,
):
    band = lax.axis_index("band")
    me = lax.axis_index("grid")
    x_at = band // 8
    y_at = lax.rem(band // 2, 4)
    core = lax.rem(band, 2)

    def at_x(x):
        return (x * 8 + y_at * 2 + core, me)

    twin = (x_at * 8 + y_at * 2 + 1 - core, me)

    def at_y(y):
        return (x_at * 8 + y * 2 + core, me)

    def at_grid(t):
        return (band, t)

    barrier = pltpu.get_barrier_semaphore()

    def hello(device):
        pl.semaphore_signal(barrier, inc=1, device_id=device, device_id_type=MESH)

    hello(twin)
    for k in range(1, 4):
        hello(at_x(lax.rem(x_at + k, 4)))
        hello(at_y(lax.rem(y_at + k, 4)))
    for k in range(1, NGRID):
        hello(at_grid(lax.rem(me + k, NGRID)))

    flat[...] = orb[...].astype(F32).reshape(NORB * SLAB, LANES)

    def classes(x, _):
        at = pl.ds(pl.multiple_of(x * 40, 8), 40)
        for m in range(5):
            for l in range(NORB):
                orbd[l, m, at, :] = flat[pl.ds(NORB * (x * 200 + m) + l, 40, stride=5 * NORB), :]
        return 0

    lax.fori_loop(0, NX, classes, 0)
    for j in range(NSRC):
        mine = [jnp.where(index[j] == NORB * band + l, 1.0, 0.0) for l in range(NORB)]

        for m in range(5):
            part = sum(mine[l] * orbd[l, m] for l in range(NORB))
            con[j, 400 * m : 400 * m + 400, :] = part.astype(BF16)
        con[j, SLAB:, :] = jnp.zeros((PADDED - SLAB, LANES), BF16)

    def granule(j, slot):
        return lax.rem(me + (NGRID - STEP) * j, NGRID) + NGRID * slot

    pl.semaphore_wait(barrier, 1 + 3 + 3 + NGRID - 1)

    def half(c):
        return pl.ds(pl.multiple_of(c * (PADDED // 2), PADDED // 2), PADDED // 2)

    def piece(x):
        return pl.ds(pl.multiple_of(x * PIECE, PIECE), PIECE)

    own = pl.ds(pl.multiple_of(core * (PADDED // 2) + x_at * PIECE, PIECE), PIECE)

    def swap(j):
        return pltpu.make_async_remote_copy(
            con.at[j, half(1 - core)], bufd.at[j], sd.at[j], rd.at[j], device_id=twin, device_id_type=MESH)

    def first(j, k):
        x = lax.rem(x_at + k, 4)
        return pltpu.make_async_remote_copy(
            pair.at[j, piece(x)], buf1.at[j, x_at], s1.at[j, k], r1.at[j],
            device_id=at_x(x), device_id_type=MESH)

    def second(j, k):
        y = lax.rem(y_at + k, 4)
        return pltpu.make_async_remote_copy(
            buf2.at[j, y_at], buf2.at[j, y_at], s2.at[j, k], r2.at[j],
            device_id=at_y(y), device_id_type=MESH)

    def third(j, k):
        x = lax.rem(x_at + k, 4)
        return pltpu.make_async_remote_copy(
            src.at[j, own], src.at[j, own], s3.at[j, k], r3.at[j],
            device_id=at_x(x), device_id_type=MESH)

    def give(j):
        ours = src.at[j, half(core)]
        return pltpu.make_async_remote_copy(
            ours, ours, se.at[j], re.at[j], device_id=twin, device_id_type=MESH)

    def along_x1(j):
        swap(j).wait_recv()
        pair[j] = (con[j, half(core), :].astype(F32) + bufd[j].astype(F32)).astype(BF16)
        for k in range(1, 4):
            first(j, k).start()
        buf1[j, x_at] = pair[j, piece(x_at), :]

    def along_y1(j):
        got = buf1.at[j, pl.ds(0, 3)]
        pltpu.make_async_copy(got, got, r1.at[j]).wait()
        buf2[j, y_at] = jnp.sum(buf1[j].astype(F32), axis=0).astype(BF16)
        for k in range(1, 4):
            second(j, k).start()

    def along_x2(j):
        got = buf2.at[j, pl.ds(0, 3)]
        pltpu.make_async_copy(got, got, r2.at[j]).wait()
        src[j, own, :] = jnp.sum(buf2[j].astype(F32), axis=0).astype(BF16)
        for k in range(1, 4):
            third(j, k).start()

    def to_twin(j):
        got = src.at[j, pl.ds(0, 3 * PIECE)]
        pltpu.make_async_copy(got, got, r3.at[j]).wait()
        give(j).start()

    swap(0).start()
    swap(1).start()
    along_x1(0)

    lane = lax.broadcasted_iota(jnp.int32, (1, LANES), 1)
    kx = squares(lax.broadcasted_iota(jnp.int32, (N, LANES), 0))
    strength = (N * SPACING) ** 2 / math.pi
    for j in range(NSRC):
        for slot in range(2):
            g = granule(j, slot)

            def fill(r, _, g=g, at=2 * j + slot):
                plain = jnp.zeros((1, LANES), jnp.int32) + (16 * lax.rem(g, GROUPS) + r)
                folded = HALF * lax.rem(lane // 32, 2) + (16 * (g - NORB * GROUPS) + r)
                rest = g >= NORB * GROUPS
                ky = jnp.where(rest, folded, plain)
                kz = jnp.where(rest, LANES + lax.rem(lane, 32), lane)
                total = kx + (squares(ky) + squares(kz))
                table[at, r] = jnp.where(total > 0, strength / (total + 1.0), 0.0)
                return 0

            lax.fori_loop(0, 16, fill, 0)

    along_y1(0)
    along_x1(1)
    along_x2(0)
    along_y1(1)
    to_twin(0)
    along_x2(1)

    zone = lax.rem(lane // 32, 2) == 0

    def order(j, k):
        turn = 2 * me + 5 * core + 3 * y_at
        low = lax.rem(7 * k + turn, NGRID)
        high = NGRID + lax.rem(2 * k + turn, GRANULES - NGRID)
        g = jnp.where(k < NGRID, low, high)
        t = lax.rem(g + STEP * j, NGRID)
        return g, t

    def forward(j, k):
        g, t = order(j, k)
        return t, pltpu.make_async_remote_copy(
            send.at[j, g], recv.at[j, g // NGRID, me], sf.at[j, k], rf.at[j, g // NGRID],
            device_id=at_grid(t), device_id_type=MESH)

    def forward_own(j, k):
        g, t = order(j, k)
        return pltpu.make_async_copy(send.at[j, g], recv.at[j, g // NGRID, me], rf.at[j, g // NGRID])

    for j in range(NSRC):
        if j == 1:
            to_twin(1)
        give(j).wait_recv()
        for m in range(5):
            wide = src[j, 400 * m : 400 * m + 400, :].astype(F32)
            for l in range(NORB):
                dens[l, m] = (wide * orbd[l, m]).astype(BF16)

        def along_z(l):
            for i in range(4):
                t = dot(dens[l, i], z_in[l, i, 0]) + dot(dens[l, i + 1], z_in[l, i, 1])
                mid[l, i] = t[:, :LANES]
                mid[NORB, i] = t[:, LANES:] if l == 0 else mid[NORB, i] + t[:, LANES:]

        def along_y(x, which):
            at = pl.ds(pl.multiple_of(x * 40, 8), 40)
            cols = [
                jnp.concatenate([mid[l, i, at, :] for i in range(4)], axis=0).astype(BF16)
                for l in which
            ]
            return dot(y_in[...], jnp.concatenate(cols, axis=1) if len(cols) > 1 else cols[0])

        def store(l, x, o, j=j):
            to = pl.ds(pl.multiple_of(x * 16, 16), 16)
            for g in range(o.shape[0] // 16):
                send[j, l * GROUPS + g, to, :] = o[16 * g : 16 * g + 16].astype(BF16)

        def post(k, _, j=j):
            t, copy = forward(j, k)

            @pl.when(t == me)
            def _():
                forward_own(j, k).start()

            @pl.when(t != me)
            def _():
                copy.start()

            return 0

        def one(x, _):
            store(0, x, along_y(x, (0,)))
            return 0

        def others(x, _):
            o = along_y(x, (1, 2))
            store(1, x, o[:, :LANES])
            last = o[:, LANES:]
            store(NORB, x, jnp.where(zone, last[:HALF], last[HALF:]))
            return 0

        along_z(0)
        lax.fori_loop(0, NX, one, 0)
        along_z(1)
        lax.fori_loop(0, NX, others, 0)
        lax.fori_loop(0, GRANULES, post, 0)

    def reply(j, slot, k):
        t = lax.rem(7 * k + 2 * me + 5 * core + 3 * y_at, NGRID)
        return t, pltpu.make_async_remote_copy(
            ready.at[j, slot, t], back.at[j, granule(j, slot)], sb.at[j, slot, k], rb.at[j],
            device_id=at_grid(t), device_id_type=MESH)

    def reply_own(j, slot):
        return pltpu.make_async_copy(ready.at[j, slot, me], back.at[j, granule(j, slot)], rb.at[j])

    def along_x(j, slot):
        got = recv.at[j, slot]
        pltpu.make_async_copy(got, got, rf.at[j, slot]).wait()
        work[...] = recv[j, slot].reshape(NGRID * PAIRROWS, LANES).astype(F32)

        def two(h, _):
            one = pl.ds(2 * h, N, stride=16)
            other = pl.ds(2 * h + 1, N, stride=16)
            f = jnp.concatenate([work[one, :].astype(BF16), work[other, :].astype(BF16)], axis=1)
            u = dot(cas[...], f)
            scale = jnp.concatenate([table[2 * j + slot, 2 * h], table[2 * j + slot, 2 * h + 1]], axis=1)
            v = dot(cas[...], (scale * u).astype(BF16))
            work[one, :] = v[:, :LANES]
            work[other, :] = v[:, LANES:]
            return 0

        lax.fori_loop(0, 8, two, 0)
        ready[j, slot] = work[...].astype(BF16).reshape(NGRID, PAIRROWS, LANES)

        def answer(k, _):
            t, copy = reply(j, slot, k)

            @pl.when(t == me)
            def _():
                reply_own(j, slot).start()

            @pl.when(t != me)
            def _():
                copy.start()

            return 0

        lax.fori_loop(0, NGRID, answer, 0)

    for j in range(NSRC):
        along_x(j, 0)

        @pl.when(granule(j, 1) < GRANULES)
        def _(j=j):
            along_x(j, 1)

    for j in range(NSRC):
        got = back.at[j]
        pltpu.make_async_copy(got, got, rb.at[j]).wait()

        def finish(l, m, value, j=j):
            value = src[j, 400 * m : 400 * m + 400, :].astype(F32) * value
            total[l, m] = value if j == 0 else total[l, m] + value

        def again_y(x, _, j=j):
            at = pl.ds(pl.multiple_of(x * 40, 8), 40)
            to = pl.ds(pl.multiple_of(x * 16, 16), 16)
            cols = [back[j, pl.ds(l * GROUPS, GROUPS), to, :].reshape(N, LANES) for l in range(NORB)]
            b = back[j, pl.ds(NORB * GROUPS, GROUPS // 2), to, :].reshape(HALF, LANES)
            turned = pltpu.roll(b.astype(F32), LANES - 32, 1).astype(BF16)
            cols.append(jnp.concatenate([b, turned], axis=0))
            o = dot(y_out[...], jnp.concatenate(cols, axis=1))
            for l in range(NORB + 1):
                for i in range(4):
                    mid[l, i, at, :] = o[40 * i : 40 * i + 40, LANES * l : LANES * (l + 1)]
            return 0

        lax.fori_loop(0, NX, again_y, 0)
        for l in range(NORB):
            left = None
            for i in range(4):
                f = jnp.concatenate([mid[l, i].astype(BF16), mid[NORB, i].astype(BF16)], axis=1)
                t = dot(f, z_out[l, i])
                here = t[:, :LANES] if left is None else left + t[:, :LANES]
                left = t[:, LANES:]
                finish(l, i, here)
            finish(l, 4, left)

    def gather(x, _):
        at = pl.ds(pl.multiple_of(x * 40, 8), 40)
        for l in range(NORB):
            for m in range(5):
                flat[pl.ds(NORB * (x * 200 + m) + l, 40, stride=5 * NORB), :] = -total[l, m, at, :]
        return 0

    lax.fori_loop(0, NX, gather, 0)
    out[...] = flat[...].reshape(SLAB, NORB, LANES).astype(BF16)

    for j in range(NSRC):
        swap(j).wait_send()
        for k in range(1, 4):
            first(j, k).wait_send()
            second(j, k).wait_send()
            third(j, k).wait_send()
        give(j).wait_send()

        def posted(k, _, j=j):
            t, copy = forward(j, k)

            @pl.when(t != me)
            def _():
                copy.wait_send()

            return 0

        lax.fori_loop(0, GRANULES, posted, 0)
        for slot in range(2):

            @pl.when(granule(j, slot) < GRANULES)
            def _(j=j, slot=slot):
                def answered(k, _):
                    t, copy = reply(j, slot, k)

                    @pl.when(t != me)
                    def _():
                        copy.wait_send()

                    return 0

                lax.fori_loop(0, NGRID, answered, 0)


def exchange(index, orb):
    consts = [jnp.asarray(t) for t in tables()]
    vmem = pl.BlockSpec(memory_space=pltpu.VMEM)
    dma = pltpu.SemaphoreType.DMA
    return pl.pallas_call(
        body,
        out_shape=jax.ShapeDtypeStruct((SLAB, NORB, LANES), BF16),
        in_specs=[pl.BlockSpec(memory_space=pltpu.SMEM)] + [vmem] * (1 + len(consts)),
        out_specs=vmem,
        scratch_shapes=[
            pltpu.VMEM((NORB * SLAB, LANES), F32),
            pltpu.VMEM((NORB, 5, 40 * NX, LANES), F32),
            pltpu.VMEM((NSRC, PADDED, LANES), BF16),
            pltpu.VMEM((NSRC, PADDED // 2, LANES), BF16),
            pltpu.VMEM((NSRC, PADDED // 2, LANES), BF16),
            pltpu.VMEM((NSRC, 4, PIECE, LANES), BF16),
            pltpu.VMEM((NSRC, 4, PIECE, LANES), BF16),
            pltpu.VMEM((NSRC, PADDED, LANES), BF16),
            pltpu.VMEM((NORB, 5, 40 * NX, LANES), BF16),
            pltpu.VMEM((NORB, 5, 40 * NX, LANES), F32),
            pltpu.VMEM((NORB + 1, 4, 40 * NX, LANES), F32),
            pltpu.VMEM((NSRC, GRANULES, PAIRROWS, LANES), BF16),
            pltpu.VMEM((NSRC, 2, NGRID, PAIRROWS, LANES), BF16),
            pltpu.VMEM((NGRID * PAIRROWS, LANES), F32),
            pltpu.VMEM((NSRC, 2, NGRID, PAIRROWS, LANES), BF16),
            pltpu.VMEM((NSRC, GRANULES, PAIRROWS, LANES), BF16),
            pltpu.VMEM((2 * NSRC, 16, N, LANES), F32),
            dma((NSRC,)),
            dma((NSRC, 4)),
            dma((NSRC, 4)),
            dma((NSRC, 4)),
            dma((NSRC,)),
            dma((NSRC, GRANULES)),
            dma((NSRC, 2, NGRID)),
            dma((NSRC,)),
            dma((NSRC,)),
            dma((NSRC,)),
            dma((NSRC,)),
            dma((NSRC,)),
            dma((NSRC, 2)),
            dma((NSRC,)),
        ],
        compiler_params=pltpu.CompilerParams(
            collective_id=0, has_side_effects=True, vmem_limit_bytes=56 << 20
        ),
        name="exchange",
    )(index, orb, *consts)


def shards(orbitals, source_index):
    rows = orbitals.reshape(NORB, SLAB, LANES).transpose(1, 0, 2)
    result = exchange(source_index, rows)
    return result.transpose(1, 0, 2).reshape(orbitals.shape)


def solution(mesh):
    return jax.shard_map(
        shards,
        mesh=mesh,
        in_specs=(P("band", "grid", None), P()),
        out_specs=P("band", "grid", None),
        check_vma=False,
    )
```

```python
import math

import jax
import jax.numpy as jnp
import ml_dtypes
import numpy as np
from jax import lax
from jax.experimental import pallas as pl
from jax.experimental.pallas import tpu as pltpu
from jax.sharding import PartitionSpec as P

MESH = pl.DeviceIdType.MESH
F32 = jnp.float32
BF16 = jnp.bfloat16

SPACING = 0.3
N = 160
NX = 10
NSRC = 2
NORB = 2
NGRID = 16
LANES = 128
REST = N - LANES
HALF = N // 2
GROUPS = N // 16
PAIRROWS = NX * 16
GRANULES = NORB * GROUPS + GROUPS // 2
SLAB = NX * N * N // LANES
PADDED = 2048
PIECE = PADDED // 8
STEP = 9


def tables():
    k = np.arange(N)
    radians = ((k[:, None] * k[None, :]) % N).astype(np.float32) * np.float32(2.0 * math.pi / N)
    cas = ((np.cos(radians) + np.sin(radians)) / np.float32(math.sqrt(N))).astype(ml_dtypes.bfloat16)
    cas = cas.astype(np.float32)
    order = np.array([4 * (r % 40) + r // 40 for r in range(N)])
    y_in = cas[:, order]
    y_out = cas[order, :]
    z_in = np.zeros((NORB, 4, 2, LANES, 2 * LANES), np.float32)
    z_out = np.zeros((NORB, 4, 2 * LANES, 2 * LANES), np.float32)
    for l in range(NORB):
        place = np.zeros((N, 2 * LANES), np.float32)
        place[:, :LANES] = cas[:, :LANES]
        for q in range(2):
            at = LANES + 64 * l + 32 * q
            place[:, at : at + REST] = cas[:, LANES:]
        back = np.zeros((2 * LANES, N), np.float32)
        back[:LANES] = cas[:LANES]
        back[LANES + 64 * l : LANES + 64 * l + REST] = cas[LANES:]
        for i in range(4):
            for part in range(2):
                for lane in range(LANES):
                    z = lane + LANES * (i + part) - N * i
                    if 0 <= z < N:
                        z_in[l, i, part, lane] = place[z]
                        z_out[l, i, :, LANES * part + lane] = back[:, z]
    return [t.astype(ml_dtypes.bfloat16) for t in (cas, y_in, y_out, z_in, z_out)]


def dot(a, b):
    return jnp.dot(a, b, preferred_element_type=F32)


def squares(index):
    folded = jnp.minimum(index, N - index).astype(F32)
    return folded * folded


def body(
    index, orb, cas, y_in, y_out, z_in, z_out, out,
    flat, orbd, con, bufd, pair, buf1, buf2, src, dens, total, mid, send, recv, work, ready, back, table,
    sd, s1, s2, s3, se, sf, sb, rd, r1, r2, r3, re, rf, rb,
):
    band = lax.axis_index("band")
    me = lax.axis_index("grid")
    x_at = band // 8
    y_at = lax.rem(band // 2, 4)
    core = lax.rem(band, 2)

    def at_x(x):
        return (x * 8 + y_at * 2 + core, me)

    twin = (x_at * 8 + y_at * 2 + 1 - core, me)

    def at_y(y):
        return (x_at * 8 + y * 2 + core, me)

    def at_grid(t):
        return (band, t)

    barrier = pltpu.get_barrier_semaphore()

    def hello(device):
        pl.semaphore_signal(barrier, inc=1, device_id=device, device_id_type=MESH)

    hello(twin)
    for k in range(1, 4):
        hello(at_x(lax.rem(x_at + k, 4)))
        hello(at_y(lax.rem(y_at + k, 4)))
    for k in range(1, NGRID):
        hello(at_grid(lax.rem(me + k, NGRID)))

    flat[...] = orb[...].astype(F32).reshape(NORB * SLAB, LANES)

    def classes(x, _):
        at = pl.ds(pl.multiple_of(x * 40, 8), 40)
        for m in range(5):
            for l in range(NORB):
                orbd[l, m, at, :] = flat[pl.ds(NORB * (x * 200 + m) + l, 40, stride=5 * NORB), :]
        return 0

    lax.fori_loop(0, NX, classes, 0)
    for j in range(NSRC):
        mine = [jnp.where(index[j] == NORB * band + l, 1.0, 0.0) for l in range(NORB)]

        for m in range(5):
            part = sum(mine[l] * orbd[l, m] for l in range(NORB))
            con[j, 400 * m : 400 * m + 400, :] = part.astype(BF16)
        con[j, SLAB:, :] = jnp.zeros((PADDED - SLAB, LANES), BF16)

    def granule(j, slot):
        return lax.rem(me + (NGRID - STEP) * j, NGRID) + NGRID * slot

    lane = lax.broadcasted_iota(jnp.int32, (1, LANES), 1)
    kx = squares(lax.broadcasted_iota(jnp.int32, (N, LANES), 0))
    strength = (N * SPACING) ** 2 / math.pi
    for j in range(NSRC):
        for slot in range(2):
            g = granule(j, slot)

            def fill(r, _, g=g, at=2 * j + slot):
                plain = jnp.zeros((1, LANES), jnp.int32) + (16 * lax.rem(g, GROUPS) + r)
                folded = HALF * lax.rem(lane // 32, 2) + (16 * (g - NORB * GROUPS) + r)
                rest = g >= NORB * GROUPS
                ky = jnp.where(rest, folded, plain)
                kz = jnp.where(rest, LANES + lax.rem(lane, 32), lane)
                total = kx + (squares(ky) + squares(kz))
                table[at, r] = jnp.where(total > 0, strength / (total + 1.0), 0.0)
                return 0

            lax.fori_loop(0, 16, fill, 0)

    pl.semaphore_wait(barrier, 1 + 3 + 3 + NGRID - 1)

    def half(c):
        return pl.ds(pl.multiple_of(c * (PADDED // 2), PADDED // 2), PADDED // 2)

    def piece(x):
        return pl.ds(pl.multiple_of(x * PIECE, PIECE), PIECE)

    own = pl.ds(pl.multiple_of(core * (PADDED // 2) + x_at * PIECE, PIECE), PIECE)

    def swap(j):
        return pltpu.make_async_remote_copy(
            con.at[j, half(1 - core)], bufd.at[j], sd.at[j], rd.at[j], device_id=twin, device_id_type=MESH)

    def first(j, k):
        x = lax.rem(x_at + k, 4)
        return pltpu.make_async_remote_copy(
            pair.at[j, piece(x)], buf1.at[j, x_at], s1.at[j, k], r1.at[j],
            device_id=at_x(x), device_id_type=MESH)

    def second(j, k):
        y = lax.rem(y_at + k, 4)
        return pltpu.make_async_remote_copy(
            buf2.at[j, y_at], buf2.at[j, y_at], s2.at[j, k], r2.at[j],
            device_id=at_y(y), device_id_type=MESH)

    def third(j, k):
        x = lax.rem(x_at + k, 4)
        return pltpu.make_async_remote_copy(
            src.at[j, own], src.at[j, own], s3.at[j, k], r3.at[j],
            device_id=at_x(x), device_id_type=MESH)

    def give(j):
        ours = src.at[j, half(core)]
        return pltpu.make_async_remote_copy(
            ours, ours, se.at[j], re.at[j], device_id=twin, device_id_type=MESH)

    def along_x1(j):
        swap(j).wait_recv()
        pair[j] = (con[j, half(core), :].astype(F32) + bufd[j].astype(F32)).astype(BF16)
        for k in range(1, 4):
            first(j, k).start()
        buf1[j, x_at] = pair[j, piece(x_at), :]

    def along_y1(j):
        got = buf1.at[j, pl.ds(0, 3)]
        pltpu.make_async_copy(got, got, r1.at[j]).wait()
        buf2[j, y_at] = jnp.sum(buf1[j].astype(F32), axis=0).astype(BF16)
        for k in range(1, 4):
            second(j, k).start()

    def along_x2(j):
        got = buf2.at[j, pl.ds(0, 3)]
        pltpu.make_async_copy(got, got, r2.at[j]).wait()
        src[j, own, :] = jnp.sum(buf2[j].astype(F32), axis=0).astype(BF16)
        for k in range(1, 4):
            third(j, k).start()

    def to_twin(j):
        got = src.at[j, pl.ds(0, 3 * PIECE)]
        pltpu.make_async_copy(got, got, r3.at[j]).wait()
        give(j).start()

    swap(0).start()
    swap(1).start()
    along_x1(0)

    along_y1(0)
    along_x1(1)
    along_x2(0)
    along_y1(1)
    to_twin(0)
    along_x2(1)

    zone = lax.rem(lane // 32, 2) == 0

    def order(j, k):
        turn = 2 * me + 5 * core + 3 * y_at
        low = lax.rem(7 * k + turn, NGRID)
        high = NGRID + lax.rem(2 * k + turn, GRANULES - NGRID)
        g = jnp.where(k < NGRID, low, high)
        t = lax.rem(g + STEP * j, NGRID)
        return g, t

    def forward(j, k):
        g, t = order(j, k)
        return t, pltpu.make_async_remote_copy(
            send.at[j, g], recv.at[j, g // NGRID, me], sf.at[j, k], rf.at[j, g // NGRID],
            device_id=at_grid(t), device_id_type=MESH)

    def forward_own(j, k):
        g, t = order(j, k)
        return pltpu.make_async_copy(send.at[j, g], recv.at[j, g // NGRID, me], rf.at[j, g // NGRID])

    for j in range(NSRC):
        if j == 1:
            to_twin(1)
        give(j).wait_recv()
        for m in range(5):
            wide = src[j, 400 * m : 400 * m + 400, :].astype(F32)
            for l in range(NORB):
                dens[l, m] = (wide * orbd[l, m]).astype(BF16)

        def along_z(l):
            for i in range(4):
                t = dot(dens[l, i], z_in[l, i, 0]) + dot(dens[l, i + 1], z_in[l, i, 1])
                mid[l, i] = t[:, :LANES]
                mid[NORB, i] = t[:, LANES:] if l == 0 else mid[NORB, i] + t[:, LANES:]

        def along_y(x, which):
            at = pl.ds(pl.multiple_of(x * 40, 8), 40)
            cols = [
                jnp.concatenate([mid[l, i, at, :] for i in range(4)], axis=0).astype(BF16)
                for l in which
            ]
            return dot(y_in[...], jnp.concatenate(cols, axis=1) if len(cols) > 1 else cols[0])

        def store(l, x, o, j=j):
            to = pl.ds(pl.multiple_of(x * 16, 16), 16)
            for g in range(o.shape[0] // 16):
                send[j, l * GROUPS + g, to, :] = o[16 * g : 16 * g + 16].astype(BF16)

        def post(k, _, j=j):
            t, copy = forward(j, k)

            @pl.when(t == me)
            def _():
                forward_own(j, k).start()

            @pl.when(t != me)
            def _():
                copy.start()

            return 0

        def one(x, _):
            store(0, x, along_y(x, (0,)))
            return 0

        def others(x, _):
            o = along_y(x, (1, 2))
            store(1, x, o[:, :LANES])
            last = o[:, LANES:]
            store(NORB, x, jnp.where(zone, last[:HALF], last[HALF:]))
            return 0

        along_z(0)
        lax.fori_loop(0, NX, one, 0)
        along_z(1)
        lax.fori_loop(0, NX, others, 0)
        lax.fori_loop(0, GRANULES, post, 0)

    def reply(j, slot, k):
        t = lax.rem(7 * k + 2 * me + 5 * core + 3 * y_at, NGRID)
        return t, pltpu.make_async_remote_copy(
            ready.at[j, slot, t], back.at[j, granule(j, slot)], sb.at[j, slot, k], rb.at[j],
            device_id=at_grid(t), device_id_type=MESH)

    def reply_own(j, slot):
        return pltpu.make_async_copy(ready.at[j, slot, me], back.at[j, granule(j, slot)], rb.at[j])

    def along_x(j, slot):
        got = recv.at[j, slot]
        pltpu.make_async_copy(got, got, rf.at[j, slot]).wait()
        work[...] = recv[j, slot].reshape(NGRID * PAIRROWS, LANES).astype(F32)

        def two(h, _):
            one = pl.ds(2 * h, N, stride=16)
            other = pl.ds(2 * h + 1, N, stride=16)
            f = jnp.concatenate([work[one, :].astype(BF16), work[other, :].astype(BF16)], axis=1)
            u = dot(cas[...], f)
            scale = jnp.concatenate([table[2 * j + slot, 2 * h], table[2 * j + slot, 2 * h + 1]], axis=1)
            v = dot(cas[...], (scale * u).astype(BF16))
            work[one, :] = v[:, :LANES]
            work[other, :] = v[:, LANES:]
            return 0

        lax.fori_loop(0, 8, two, 0)
        ready[j, slot] = work[...].astype(BF16).reshape(NGRID, PAIRROWS, LANES)

        def answer(k, _):
            t, copy = reply(j, slot, k)

            @pl.when(t == me)
            def _():
                reply_own(j, slot).start()

            @pl.when(t != me)
            def _():
                copy.start()

            return 0

        lax.fori_loop(0, NGRID, answer, 0)

    for j in range(NSRC):
        along_x(j, 0)

        @pl.when(granule(j, 1) < GRANULES)
        def _(j=j):
            along_x(j, 1)

    for j in range(NSRC):
        got = back.at[j]
        pltpu.make_async_copy(got, got, rb.at[j]).wait()

        def finish(l, m, value, j=j):
            value = src[j, 400 * m : 400 * m + 400, :].astype(F32) * value
            total[l, m] = value if j == 0 else total[l, m] + value

        def again_y(x, _, j=j):
            at = pl.ds(pl.multiple_of(x * 40, 8), 40)
            to = pl.ds(pl.multiple_of(x * 16, 16), 16)
            cols = [back[j, pl.ds(l * GROUPS, GROUPS), to, :].reshape(N, LANES) for l in range(NORB)]
            b = back[j, pl.ds(NORB * GROUPS, GROUPS // 2), to, :].reshape(HALF, LANES)
            turned = pltpu.roll(b.astype(F32), LANES - 32, 1).astype(BF16)
            cols.append(jnp.concatenate([b, turned], axis=0))
            o = dot(y_out[...], jnp.concatenate(cols, axis=1))
            for l in range(NORB + 1):
                for i in range(4):
                    mid[l, i, at, :] = o[40 * i : 40 * i + 40, LANES * l : LANES * (l + 1)]
            return 0

        lax.fori_loop(0, NX, again_y, 0)
        for l in range(NORB):
            left = None
            for i in range(4):
                f = jnp.concatenate([mid[l, i].astype(BF16), mid[NORB, i].astype(BF16)], axis=1)
                t = dot(f, z_out[l, i])
                here = t[:, :LANES] if left is None else left + t[:, :LANES]
                left = t[:, LANES:]
                finish(l, i, here)
            finish(l, 4, left)

    def gather(x, _):
        at = pl.ds(pl.multiple_of(x * 40, 8), 40)
        for l in range(NORB):
            for m in range(5):
                flat[pl.ds(NORB * (x * 200 + m) + l, 40, stride=5 * NORB), :] = -total[l, m, at, :]
        return 0

    lax.fori_loop(0, NX, gather, 0)
    out[...] = flat[...].reshape(SLAB, NORB, LANES).astype(BF16)

    for j in range(NSRC):
        swap(j).wait_send()
        for k in range(1, 4):
            first(j, k).wait_send()
            second(j, k).wait_send()
            third(j, k).wait_send()
        give(j).wait_send()

        def posted(k, _, j=j):
            t, copy = forward(j, k)

            @pl.when(t != me)
            def _():
                copy.wait_send()

            return 0

        lax.fori_loop(0, GRANULES, posted, 0)
        for slot in range(2):

            @pl.when(granule(j, slot) < GRANULES)
            def _(j=j, slot=slot):
                def answered(k, _):
                    t, copy = reply(j, slot, k)

                    @pl.when(t != me)
                    def _():
                        copy.wait_send()

                    return 0

                lax.fori_loop(0, NGRID, answered, 0)


def exchange(index, orb):
    consts = [jnp.asarray(t) for t in tables()]
    vmem = pl.BlockSpec(memory_space=pltpu.VMEM)
    dma = pltpu.SemaphoreType.DMA
    return pl.pallas_call(
        body,
        out_shape=jax.ShapeDtypeStruct((SLAB, NORB, LANES), BF16),
        in_specs=[pl.BlockSpec(memory_space=pltpu.SMEM)] + [vmem] * (1 + len(consts)),
        out_specs=vmem,
        scratch_shapes=[
            pltpu.VMEM((NORB * SLAB, LANES), F32),
            pltpu.VMEM((NORB, 5, 40 * NX, LANES), F32),
            pltpu.VMEM((NSRC, PADDED, LANES), BF16),
            pltpu.VMEM((NSRC, PADDED // 2, LANES), BF16),
            pltpu.VMEM((NSRC, PADDED // 2, LANES), BF16),
            pltpu.VMEM((NSRC, 4, PIECE, LANES), BF16),
            pltpu.VMEM((NSRC, 4, PIECE, LANES), BF16),
            pltpu.VMEM((NSRC, PADDED, LANES), BF16),
            pltpu.VMEM((NORB, 5, 40 * NX, LANES), BF16),
            pltpu.VMEM((NORB, 5, 40 * NX, LANES), F32),
            pltpu.VMEM((NORB + 1, 4, 40 * NX, LANES), F32),
            pltpu.VMEM((NSRC, GRANULES, PAIRROWS, LANES), BF16),
            pltpu.VMEM((NSRC, 2, NGRID, PAIRROWS, LANES), BF16),
            pltpu.VMEM((NGRID * PAIRROWS, LANES), F32),
            pltpu.VMEM((NSRC, 2, NGRID, PAIRROWS, LANES), BF16),
            pltpu.VMEM((NSRC, GRANULES, PAIRROWS, LANES), BF16),
            pltpu.VMEM((2 * NSRC, 16, N, LANES), F32),
            dma((NSRC,)),
            dma((NSRC, 4)),
            dma((NSRC, 4)),
            dma((NSRC, 4)),
            dma((NSRC,)),
            dma((NSRC, GRANULES)),
            dma((NSRC, 2, NGRID)),
            dma((NSRC,)),
            dma((NSRC,)),
            dma((NSRC,)),
            dma((NSRC,)),
            dma((NSRC,)),
            dma((NSRC, 2)),
            dma((NSRC,)),
        ],
        compiler_params=pltpu.CompilerParams(
            collective_id=0, has_side_effects=True, vmem_limit_bytes=56 << 20
        ),
        name="exchange",
    )(index, orb, *consts)


def shards(orbitals, source_index):
    rows = orbitals.reshape(NORB, SLAB, LANES).transpose(1, 0, 2)
    result = exchange(source_index, rows)
    return result.transpose(1, 0, 2).reshape(orbitals.shape)


def solution(mesh):
    return jax.shard_map(
        shards,
        mesh=mesh,
        in_specs=(P("band", "grid", None), P()),
        out_specs=P("band", "grid", None),
        check_vma=False,
    )
```

```python
import math

import jax
import jax.numpy as jnp
import ml_dtypes
import numpy as np
from jax import lax
from jax.experimental import pallas as pl
from jax.experimental.pallas import tpu as pltpu
from jax.sharding import PartitionSpec as P

MESH = pl.DeviceIdType.MESH
F32 = jnp.float32
BF16 = jnp.bfloat16

SPACING = 0.3
N = 160
NX = 10
NSRC = 2
NORB = 2
NGRID = 16
LANES = 128
REST = N - LANES
HALF = N // 2
GROUPS = N // 16
PAIRROWS = NX * 16
GRANULES = NORB * GROUPS + GROUPS // 2
SLAB = NX * N * N // LANES
PADDED = 2048
PIECE = PADDED // 8
STEP = 9


def tables():
    k = np.arange(N)
    radians = ((k[:, None] * k[None, :]) % N).astype(np.float32) * np.float32(2.0 * math.pi / N)
    cas = ((np.cos(radians) + np.sin(radians)) / np.float32(math.sqrt(N))).astype(ml_dtypes.bfloat16)
    cas = cas.astype(np.float32)
    order = np.array([4 * (r % 40) + r // 40 for r in range(N)])
    y_in = cas[:, order]
    y_out = cas[order, :]
    z_in = np.zeros((NORB, 4, 2, LANES, 2 * LANES), np.float32)
    z_out = np.zeros((NORB, 4, 2 * LANES, 2 * LANES), np.float32)
    for l in range(NORB):
        place = np.zeros((N, 2 * LANES), np.float32)
        place[:, :LANES] = cas[:, :LANES]
        for q in range(2):
            at = LANES + 64 * l + 32 * q
            place[:, at : at + REST] = cas[:, LANES:]
        back = np.zeros((2 * LANES, N), np.float32)
        back[:LANES] = cas[:LANES]
        back[LANES + 64 * l : LANES + 64 * l + REST] = cas[LANES:]
        for i in range(4):
            for part in range(2):
                for lane in range(LANES):
                    z = lane + LANES * (i + part) - N * i
                    if 0 <= z < N:
                        z_in[l, i, part, lane] = place[z]
                        z_out[l, i, :, LANES * part + lane] = back[:, z]
    return [t.astype(ml_dtypes.bfloat16) for t in (cas, y_in, y_out, z_in, z_out)]


def dot(a, b):
    return jnp.dot(a, b, preferred_element_type=F32)


def squares(index):
    folded = jnp.minimum(index, N - index).astype(F32)
    return folded * folded


def body(
    index, orb, cas, y_in, y_out, z_in, z_out, out,
    flat, orbd, con, bufd, pair, buf1, buf2, src, dens, total, mid, send, recv, work, ready, back, table,
    sd, s1, s2, s3, se, sf, sb, rd, r1, r2, r3, re, rf, rb,
):
    band = lax.axis_index("band")
    me = lax.axis_index("grid")
    x_at = band // 8
    y_at = lax.rem(band // 2, 4)
    core = lax.rem(band, 2)

    def at_x(x):
        return (x * 8 + y_at * 2 + core, me)

    twin = (x_at * 8 + y_at * 2 + 1 - core, me)

    def at_y(y):
        return (x_at * 8 + y * 2 + core, me)

    def at_grid(t):
        return (band, t)

    barrier = pltpu.get_barrier_semaphore()

    def hello(device):
        pl.semaphore_signal(barrier, inc=1, device_id=device, device_id_type=MESH)

    hello(twin)
    for k in range(1, 4):
        hello(at_x(lax.rem(x_at + k, 4)))
        hello(at_y(lax.rem(y_at + k, 4)))
    for k in range(1, NGRID):
        hello(at_grid(lax.rem(me + k, NGRID)))

    flat[...] = orb[...].astype(F32).reshape(NORB * SLAB, LANES)

    def classes(x, _):
        at = pl.ds(pl.multiple_of(x * 40, 8), 40)
        for m in range(5):
            for l in range(NORB):
                orbd[l, m, at, :] = flat[pl.ds(NORB * (x * 200 + m) + l, 40, stride=5 * NORB), :]
        return 0

    lax.fori_loop(0, NX, classes, 0)
    for j in range(NSRC):
        mine = [jnp.where(index[j] == NORB * band + l, 1.0, 0.0) for l in range(NORB)]

        for m in range(5):
            part = sum(mine[l] * orbd[l, m] for l in range(NORB))
            con[j, 400 * m : 400 * m + 400, :] = part.astype(BF16)
        con[j, SLAB:, :] = jnp.zeros((PADDED - SLAB, LANES), BF16)

    def granule(j, slot):
        return lax.rem(me + (NGRID - STEP) * j, NGRID) + NGRID * slot

    lane = lax.broadcasted_iota(jnp.int32, (1, LANES), 1)
    kx = squares(lax.broadcasted_iota(jnp.int32, (N, LANES), 0))
    strength = (N * SPACING) ** 2 / math.pi
    for j in range(NSRC):
        for slot in range(2):
            g = granule(j, slot)

            def fill(r, _, g=g, at=2 * j + slot):
                plain = jnp.zeros((1, LANES), jnp.int32) + (16 * lax.rem(g, GROUPS) + r)
                folded = HALF * lax.rem(lane // 32, 2) + (16 * (g - NORB * GROUPS) + r)
                rest = g >= NORB * GROUPS
                ky = jnp.where(rest, folded, plain)
                kz = jnp.where(rest, LANES + lax.rem(lane, 32), lane)
                total = kx + (squares(ky) + squares(kz))
                table[at, r] = jnp.where(total > 0, strength / (total + 1.0), 0.0)
                return 0

            lax.fori_loop(0, 16, fill, 0)

    pl.semaphore_wait(barrier, 1 + 3 + 3 + NGRID - 1)

    def half(c):
        return pl.ds(pl.multiple_of(c * (PADDED // 2), PADDED // 2), PADDED // 2)

    def piece(x):
        return pl.ds(pl.multiple_of(x * PIECE, PIECE), PIECE)

    own = pl.ds(pl.multiple_of(core * (PADDED // 2) + x_at * PIECE, PIECE), PIECE)

    def swap(j):
        return pltpu.make_async_remote_copy(
            con.at[j, half(1 - core)], bufd.at[j], sd.at[j], rd.at[j], device_id=twin, device_id_type=MESH)

    def first(j, k):
        x = lax.rem(x_at + k, 4)
        return pltpu.make_async_remote_copy(
            pair.at[j, piece(x)], buf1.at[j, x_at], s1.at[j, k], r1.at[j],
            device_id=at_x(x), device_id_type=MESH)

    def second(j, k):
        y = lax.rem(y_at + k, 4)
        return pltpu.make_async_remote_copy(
            buf2.at[j, y_at], buf2.at[j, y_at], s2.at[j, k], r2.at[j],
            device_id=at_y(y), device_id_type=MESH)

    def third(j, k):
        x = lax.rem(x_at + k, 4)
        return pltpu.make_async_remote_copy(
            src.at[j, own], src.at[j, own], s3.at[j, k], r3.at[j],
            device_id=at_x(x), device_id_type=MESH)

    def give(j):
        ours = src.at[j, half(core)]
        return pltpu.make_async_remote_copy(
            ours, ours, se.at[j], re.at[j], device_id=twin, device_id_type=MESH)

    def along_x1(j):
        swap(j).wait_recv()
        pair[j] = (con[j, half(core), :].astype(F32) + bufd[j].astype(F32)).astype(BF16)
        for k in range(1, 4):
            first(j, k).start()
        buf1[j, x_at] = pair[j, piece(x_at), :]

    def along_y1(j):
        got = buf1.at[j, pl.ds(0, 3)]
        pltpu.make_async_copy(got, got, r1.at[j]).wait()
        buf2[j, y_at] = jnp.sum(buf1[j].astype(F32), axis=0).astype(BF16)
        for k in range(1, 4):
            second(j, k).start()

    def along_x2(j):
        got = buf2.at[j, pl.ds(0, 3)]
        pltpu.make_async_copy(got, got, r2.at[j]).wait()
        src[j, own, :] = jnp.sum(buf2[j].astype(F32), axis=0).astype(BF16)
        for k in range(1, 4):
            third(j, k).start()

    def to_twin(j):
        got = src.at[j, pl.ds(0, 3 * PIECE)]
        pltpu.make_async_copy(got, got, r3.at[j]).wait()
        give(j).start()

    swap(0).start()
    swap(1).start()
    along_x1(0)

    along_y1(0)
    along_x1(1)
    along_x2(0)
    along_y1(1)
    to_twin(0)
    along_x2(1)

    zone = lax.rem(lane // 32, 2) == 0

    def order(j, k):
        turn = 2 * me + 5 * core + 3 * y_at
        low = lax.rem(7 * k + turn, NGRID)
        high = NGRID + lax.rem(2 * k + turn, GRANULES - NGRID)
        g = jnp.where(k < NGRID, low, high)
        t = lax.rem(g + STEP * j, NGRID)
        return g, t

    def forward(j, k):
        g, t = order(j, k)
        return t, pltpu.make_async_remote_copy(
            send.at[j, g], recv.at[j, g // NGRID, me], sf.at[j, k], rf.at[j, g // NGRID],
            device_id=at_grid(t), device_id_type=MESH)

    def forward_own(j, k):
        g, t = order(j, k)
        return pltpu.make_async_copy(send.at[j, g], recv.at[j, g // NGRID, me], rf.at[j, g // NGRID])

    for j in range(NSRC):
        if j == 1:
            to_twin(1)
        give(j).wait_recv()
        for m in range(5):
            wide = src[j, 400 * m : 400 * m + 400, :].astype(F32)
            for l in range(NORB):
                dens[l, m] = (wide * orbd[l, m]).astype(BF16)

        def along_z(l):
            for i in range(4):
                t = dot(dens[l, i], z_in[l, i, 0]) + dot(dens[l, i + 1], z_in[l, i, 1])
                mid[l, i] = t[:, :LANES]
                mid[NORB, i] = t[:, LANES:] if l == 0 else mid[NORB, i] + t[:, LANES:]

        def along_y(x, which):
            at = pl.ds(pl.multiple_of(x * 40, 8), 40)
            cols = [
                jnp.concatenate([mid[l, i, at, :] for i in range(4)], axis=0).astype(BF16)
                for l in which
            ]
            return dot(y_in[...], jnp.concatenate(cols, axis=1) if len(cols) > 1 else cols[0])

        def store(l, x, o, j=j):
            to = pl.ds(pl.multiple_of(x * 16, 16), 16)
            for g in range(o.shape[0] // 16):
                send[j, l * GROUPS + g, to, :] = o[16 * g : 16 * g + 16].astype(BF16)

        def post(k, _, j=j):
            t, copy = forward(j, k)

            @pl.when(t == me)
            def _():
                forward_own(j, k).start()

            @pl.when(t != me)
            def _():
                copy.start()

            return 0

        def one(x, _):
            store(0, x, along_y(x, (0,)))
            return 0

        def others(x, _):
            o = along_y(x, (1, 2))
            store(1, x, o[:, :LANES])
            last = o[:, LANES:]
            store(NORB, x, jnp.where(zone, last[:HALF], last[HALF:]))
            return 0

        along_z(0)
        lax.fori_loop(0, NX, one, 0)
        along_z(1)
        lax.fori_loop(0, NX, others, 0)
        lax.fori_loop(0, GRANULES, post, 0)

    def reply(j, slot, k):
        t = lax.rem(7 * k + 2 * me + 5 * core + 3 * y_at, NGRID)
        return t, pltpu.make_async_remote_copy(
            ready.at[j, slot, t], back.at[j, granule(j, slot)], sb.at[j, slot, k], rb.at[j],
            device_id=at_grid(t), device_id_type=MESH)

    def reply_own(j, slot):
        return pltpu.make_async_copy(ready.at[j, slot, me], back.at[j, granule(j, slot)], rb.at[j])

    def along_x(j, slot):
        got = recv.at[j, slot]
        pltpu.make_async_copy(got, got, rf.at[j, slot]).wait()
        work[...] = recv[j, slot].reshape(NGRID * PAIRROWS, LANES).astype(F32)

        def two(h, _):
            one = pl.ds(2 * h, N, stride=16)
            other = pl.ds(2 * h + 1, N, stride=16)
            f = jnp.concatenate([work[one, :].astype(BF16), work[other, :].astype(BF16)], axis=1)
            u = dot(cas[...], f)
            scale = jnp.concatenate([table[2 * j + slot, 2 * h], table[2 * j + slot, 2 * h + 1]], axis=1)
            v = dot(cas[...], (scale * u).astype(BF16))
            work[one, :] = v[:, :LANES]
            work[other, :] = v[:, LANES:]
            return 0

        lax.fori_loop(0, 8, two, 0)
        ready[j, slot] = work[...].astype(BF16).reshape(NGRID, PAIRROWS, LANES)

        def answer(k, _):
            t, copy = reply(j, slot, k)

            @pl.when(t == me)
            def _():
                reply_own(j, slot).start()

            @pl.when(t != me)
            def _():
                copy.start()

            return 0

        lax.fori_loop(0, NGRID, answer, 0)

    for j in range(NSRC):
        along_x(j, 0)

        @pl.when(granule(j, 1) < GRANULES)
        def _(j=j):
            along_x(j, 1)

    for j in range(NSRC):
        got = back.at[j]
        pltpu.make_async_copy(got, got, rb.at[j]).wait()

        def finish(l, m, value, j=j):
            value = src[j, 400 * m : 400 * m + 400, :].astype(F32) * value
            total[l, m] = value if j == 0 else total[l, m] + value

        def again_y(x, _, j=j):
            at = pl.ds(pl.multiple_of(x * 40, 8), 40)
            to = pl.ds(pl.multiple_of(x * 16, 16), 16)
            cols = [back[j, pl.ds(l * GROUPS, GROUPS), to, :].reshape(N, LANES) for l in range(NORB)]
            b = back[j, pl.ds(NORB * GROUPS, GROUPS // 2), to, :].reshape(HALF, LANES)
            turned = pltpu.roll(b.astype(F32), LANES - 32, 1).astype(BF16)
            cols.append(jnp.concatenate([b, turned], axis=0))
            o = dot(y_out[...], jnp.concatenate(cols, axis=1))
            for l in range(NORB + 1):
                for i in range(4):
                    mid[l, i, at, :] = o[40 * i : 40 * i + 40, LANES * l : LANES * (l + 1)]
            return 0

        lax.fori_loop(0, NX, again_y, 0)
        for l in range(NORB):
            left = None
            for i in range(4):
                f = jnp.concatenate([mid[l, i].astype(BF16), mid[NORB, i].astype(BF16)], axis=1)
                t = dot(f, z_out[l, i])
                here = t[:, :LANES] if left is None else left + t[:, :LANES]
                left = t[:, LANES:]
                finish(l, i, here)
            finish(l, 4, left)

    def gather(x, _):
        at = pl.ds(pl.multiple_of(x * 40, 8), 40)
        for l in range(NORB):
            for m in range(5):
                flat[pl.ds(NORB * (x * 200 + m) + l, 40, stride=5 * NORB), :] = total[l, m, at, :]
        return 0

    lax.fori_loop(0, NX, gather, 0)
    out[...] = flat[...].reshape(SLAB, NORB, LANES).astype(BF16)

    for j in range(NSRC):
        swap(j).wait_send()
        for k in range(1, 4):
            first(j, k).wait_send()
            second(j, k).wait_send()
            third(j, k).wait_send()
        give(j).wait_send()

        def posted(k, _, j=j):
            t, copy = forward(j, k)

            @pl.when(t != me)
            def _():
                copy.wait_send()

            return 0

        lax.fori_loop(0, GRANULES, posted, 0)
        for slot in range(2):

            @pl.when(granule(j, slot) < GRANULES)
            def _(j=j, slot=slot):
                def answered(k, _):
                    t, copy = reply(j, slot, k)

                    @pl.when(t != me)
                    def _():
                        copy.wait_send()

                    return 0

                lax.fori_loop(0, NGRID, answered, 0)


def exchange(index, orb):
    consts = [jnp.asarray(t) for t in tables()]
    vmem = pl.BlockSpec(memory_space=pltpu.VMEM)
    dma = pltpu.SemaphoreType.DMA
    return pl.pallas_call(
        body,
        out_shape=jax.ShapeDtypeStruct((SLAB, NORB, LANES), BF16),
        in_specs=[pl.BlockSpec(memory_space=pltpu.SMEM)] + [vmem] * (1 + len(consts)),
        out_specs=vmem,
        scratch_shapes=[
            pltpu.VMEM((NORB * SLAB, LANES), F32),
            pltpu.VMEM((NORB, 5, 40 * NX, LANES), F32),
            pltpu.VMEM((NSRC, PADDED, LANES), BF16),
            pltpu.VMEM((NSRC, PADDED // 2, LANES), BF16),
            pltpu.VMEM((NSRC, PADDED // 2, LANES), BF16),
            pltpu.VMEM((NSRC, 4, PIECE, LANES), BF16),
            pltpu.VMEM((NSRC, 4, PIECE, LANES), BF16),
            pltpu.VMEM((NSRC, PADDED, LANES), BF16),
            pltpu.VMEM((NORB, 5, 40 * NX, LANES), BF16),
            pltpu.VMEM((NORB, 5, 40 * NX, LANES), F32),
            pltpu.VMEM((NORB + 1, 4, 40 * NX, LANES), F32),
            pltpu.VMEM((NSRC, GRANULES, PAIRROWS, LANES), BF16),
            pltpu.VMEM((NSRC, 2, NGRID, PAIRROWS, LANES), BF16),
            pltpu.VMEM((NGRID * PAIRROWS, LANES), F32),
            pltpu.VMEM((NSRC, 2, NGRID, PAIRROWS, LANES), BF16),
            pltpu.VMEM((NSRC, GRANULES, PAIRROWS, LANES), BF16),
            pltpu.VMEM((2 * NSRC, 16, N, LANES), F32),
            dma((NSRC,)),
            dma((NSRC, 4)),
            dma((NSRC, 4)),
            dma((NSRC, 4)),
            dma((NSRC,)),
            dma((NSRC, GRANULES)),
            dma((NSRC, 2, NGRID)),
            dma((NSRC,)),
            dma((NSRC,)),
            dma((NSRC,)),
            dma((NSRC,)),
            dma((NSRC,)),
            dma((NSRC, 2)),
            dma((NSRC,)),
        ],
        compiler_params=pltpu.CompilerParams(
            collective_id=0, has_side_effects=True, vmem_limit_bytes=56 << 20
        ),
        name="exchange",
    )(index, orb, *consts)


def shards(orbitals, source_index):
    rows = orbitals.reshape(NORB, SLAB, LANES).transpose(1, 0, 2)
    result = exchange(source_index, rows)
    return -result.transpose(1, 0, 2).reshape(orbitals.shape)


def solution(mesh):
    return jax.shard_map(
        shards,
        mesh=mesh,
        in_specs=(P("band", "grid", None), P()),
        out_specs=P("band", "grid", None),
        check_vma=False,
    )
```
